512 devices in a mesh: group: 64 (over x, z, core), head: 8 (over y).
Axes of the slice: x: 4, y: 8, z: 8, core: 2. Of those that a mesh axis runs over, the one named last changes fastest.
Arguments:
- tokens: bfloat16 [16384, 3072], P(('group', 'head')), may hold values from -10 to 10
- attn_gain: float32 [3072], replicated, may hold values from 0.25 to 1.75
- w_query: bfloat16 [3072, 1536], P('group', 'head'), may hold values from -1 to 1
- w_key: bfloat16 [3072, 1536], P('group', 'head'), may hold values from -1 to 1
- w_value: bfloat16 [3072, 1536], P('group', 'head'), may hold values from -0.109375 to 0.109375
- w_out: bfloat16 [1536, 3072], P('head', 'group'), may hold values from -0.15625 to 0.15625
- mlp_gain: float32 [3072], replicated, may hold values from 0.25 to 1.75
- w_gate: bfloat16 [3072, 4096], P('group', 'head'), may hold values from -0.109375 to 0.109375
- w_up: bfloat16 [3072, 4096], P('group', 'head'), may hold values from -0.109375 to 0.109375
- w_down: bfloat16 [4096, 3072], P('head', 'group'), may hold values from -0.09375 to 0.09375
- segment_ids: int32 [64, 256], P('group'), may hold values from 0 to 3, never falling along the last dimension, each value on 1 to 128 neighbouring positions
- cache_slot: int32 [64, 256], P('group'), may hold values from 0 to 255, each once within a row
Outputs:
- layer_out: bfloat16 [16384, 3072], P(('group', 'head'))
- cache_keys: bfloat16 [16384, 1536], P('group', 'head')
- cache_values: bfloat16 [16384, 1536], P('group', 'head')
The draws below stay inside these ranges and needn't reach their ends.
Inputs may be any that keep to these rules, and one draw needn't show every extreme that they name: `segment_ids`: within each group, segment ids never fall; each of the 4 prompts has 1 to 128 tokens and one has exactly 128. `cache_slot`: each group's row of cache slots holds every slot once.
All inputs are finite; a program needn't handle non-finite values.
Results may differ from the reference program's by a relative error of at most 0.018.
Values may be sent and summed in bfloat16 or wider, within the bound.
A program may use at most 64 MiB of HBM per device.

```python
import math
import jax
import jax.numpy as jnp
import numpy as np
from jax import lax

D = 3072
HEAD_DIM = 96
HEADS = 16
FFW = 4096
SEGS = 4
GROUPS = 64
GRP_TOK = 256
TOKENS = 16384
SEG_MOST = 128
N_HEAD = 8


def drawn_weight(key, salt):
    noise = jax.random.truncated_normal(jax.random.fold_in(key, salt), -6.0, 6.0, (D, HEADS * HEAD_DIM), jnp.float32)
    weight = noise * float(D) ** (-0.5)
    return weight


def draw_w_query(key, part):
    return drawn_weight(key, 101).astype(jnp.bfloat16)


def draw_w_key(key, part):
    return drawn_weight(key, 102).astype(jnp.bfloat16)


def draw_tokens(key, part):
    noise = jax.random.truncated_normal(jax.random.fold_in(key, 103), -6.0, 6.0, (TOKENS, D), jnp.float32)
    return noise.astype(jnp.bfloat16)


def levels(stream_key, shape, pieces, smallest, largest):
    def one(dim, parts):
        heights = jax.random.uniform(jax.random.fold_in(jax.random.fold_in(stream_key, 6), dim), (parts,), jnp.float32, smallest / len(pieces), largest / len(pieces))
        return jnp.repeat(jnp.exp(heights), shape[dim] // parts).reshape((-1,) + (1,) * (len(shape) - dim - 1))

    factor_of = one(*pieces[0])
    for cut in pieces[1:]:
        factor_of = factor_of * one(*cut)
    return factor_of


def length_profile(count, total, most, skew):
    loads = [(1 << 20) // math.isqrt(rank ** skew) + 1 for rank in range(2, count + 1)]
    spare, holding = total - most - (count - 1), [1] * (count - 1)
    while spare > 0:
        movable = [i for i in range(count - 1) if holding[i] < most]
        whole, remaining = sum([loads[i] for i in movable]), spare
        for i in movable:
            extra = min(most - holding[i], max(1, remaining * loads[i] // whole), spare)
            holding[i] = holding[i] + extra
            spare = spare - extra
    return np.array([most] + holding)


def ragged(stream_key, amount, total, most, lean):
    if amount == 2:
        one = jax.random.randint(stream_key, (), max(1, total - most), min(most, total - 1) + 1)
        return jnp.stack([one, total - one])
    tallies = jnp.asarray(length_profile(amount, total, most, lean), jnp.int32)
    twos = (amount - 1) // 2
    giver, sink = tallies[1:1 + 2 * twos:2], tallies[2:2 + 2 * twos:2]
    room = jnp.minimum(giver - 1, most - sink)
    shifted = jax.random.randint(jax.random.fold_in(stream_key, 1), (twos,), 0, 1 << 20) % (room + 1)
    tallies = tallies.at[1:1 + 2 * twos:2].set(giver - shifted).at[2:2 + 2 * twos:2].set(sink + shifted)
    return tallies[jax.random.permutation(jax.random.fold_in(stream_key, 2), amount)]


def normal_values(key, dims, deviation, reach, shards=(), kind=jnp.bfloat16):
    entries = jax.random.normal(key, dims, jnp.float32) * deviation
    if len(shards) > 0:
        entries = levels(key, dims, shards, -0.22, 0.18) * entries
    return jnp.clip(entries, min=-reach, max=reach).astype(kind)


def setup_inputs(seed: int = 0) -> dict:
    arg_keys = jax.random.split(jax.random.key(seed), 13)
    return {
        "tokens": draw_tokens(jax.random.fold_in(arg_keys[12], 71), 0),
        "attn_gain": jnp.clip(1.0 + 0.15 * jax.random.normal(arg_keys[1], (D,), jnp.float32), 0.25, 1.75),
        "w_query": draw_w_query(jax.random.fold_in(arg_keys[12], 71), 0),
        "w_key": draw_w_key(jax.random.fold_in(arg_keys[12], 71), 0),
        "w_value": normal_values(arg_keys[4], (D, HEADS * HEAD_DIM), D ** -0.5, 0.109375, ((0, 64), (1, 8))),
        "w_out": normal_values(arg_keys[5], (HEADS * HEAD_DIM, D), (HEADS * HEAD_DIM) ** -0.5, 0.15625, ((0, 8), (1, 64))),
        "mlp_gain": jnp.clip(1.0 + 0.15 * jax.random.normal(arg_keys[6], (D,), jnp.float32), 0.25, 1.75),
        "w_gate": normal_values(arg_keys[7], (D, FFW), D ** -0.5, 0.109375, ((0, 64), (1, 8))),
        "w_up": normal_values(arg_keys[8], (D, FFW), D ** -0.5, 0.109375, ((0, 64), (1, 8))),
        "w_down": normal_values(arg_keys[9], (FFW, D), FFW ** -0.5, 0.09375, ((0, 8), (1, 64))),
        "segment_ids": jax.vmap(lambda own: jnp.searchsorted(jnp.cumsum(ragged(own, SEGS, GRP_TOK, SEG_MOST, 2)), jnp.arange(GRP_TOK), side="right"))(jax.random.split(arg_keys[10], GROUPS)).reshape((GROUPS, GRP_TOK)).astype(jnp.int32),
        "cache_slot": jax.vmap(lambda own: jax.random.permutation(own, GRP_TOK))(jax.random.split(arg_keys[11], GROUPS)).reshape((GROUPS, GRP_TOK)).astype(jnp.int32),
    }


def norm_rows(rows, gain):
    values = rows.astype(jnp.float32)
    scale = lax.rsqrt(lax.optimization_barrier(jnp.mean(values * values, axis=-1, keepdims=True)) + 1e-05)
    return (values * scale * gain.astype(jnp.float32)).astype(jnp.bfloat16)

def positions(segment):
    count = segment.shape[0]
    index = jnp.arange(count, dtype=jnp.int32)
    before = jnp.concatenate([jnp.full((1,), -1, jnp.int32), segment[:-1].astype(jnp.int32)])
    starts = jnp.where(segment.astype(jnp.int32) != before, index, jnp.zeros_like(index))
    return index - lax.cummax(starts, axis=0)

def rotate(heads, place):
    half = heads.shape[-1] // 2
    freq = 10000.0 ** (-2.0 * jnp.arange(half, dtype=jnp.float32) / heads.shape[-1])
    angle = place.astype(jnp.float32)[:, None] * freq[None, :]
    cosine = jnp.cos(angle)[:, None, :]
    sine = jnp.sin(angle)[:, None, :]
    first = heads[..., :half]
    second = heads[..., half:]
    return jnp.concatenate([first * cosine - second * sine, second * cosine + first * sine], axis=-1)

def attend_group(inputs):
    query, key, value, segment = inputs
    count = segment.shape[0]
    index = jnp.arange(count, dtype=jnp.int32)
    allowed = (segment[:, None] == segment[None, :]) & (index[None, :] <= index[:, None])
    scores = jnp.einsum('qhd,khd->hqk', query.astype(jnp.float32), key.astype(jnp.float32))
    scores = scores * (1.0 / HEAD_DIM ** 0.5)
    scores = jnp.where(allowed[None, :, :], scores, -1e+30)
    top = lax.optimization_barrier(jnp.max(scores, axis=-1, keepdims=True))
    expo = jnp.exp(scores - top)
    probs = (expo / lax.optimization_barrier(jnp.sum(expo, axis=-1, keepdims=True))).astype(jnp.bfloat16)
    mixed = jnp.einsum('hqk,khd->qhd', probs.astype(jnp.float32), value.astype(jnp.float32))
    return mixed.astype(jnp.bfloat16)

def place_cache(rows, slots):
    return jnp.zeros_like(rows).at[slots].set(rows)

def block_sum(left, right, blocks):
    width = left.shape[1] // blocks
    total = jnp.zeros((left.shape[0], right.shape[1]), jnp.float32)
    for block in range(blocks):
        part = jnp.dot(left[:, block * width:(block + 1) * width], right[block * width:(block + 1) * width, :], preferred_element_type=jnp.float32)
        total = total + lax.optimization_barrier(part.astype(jnp.bfloat16)).astype(jnp.float32)
    return total

def reference(tokens, attn_gain, w_query, w_key, w_value, w_out, mlp_gain, w_gate, w_up, w_down, segment_ids, cache_slot):
    normed = norm_rows(tokens, attn_gain)
    query = jnp.dot(normed, w_query, preferred_element_type=jnp.float32)
    key = jnp.dot(normed, w_key, preferred_element_type=jnp.float32)
    value = jnp.dot(normed, w_value, preferred_element_type=jnp.float32)
    place = jax.vmap(positions)(segment_ids).reshape(-1)
    q_rot = rotate(query.reshape(TOKENS, HEADS, HEAD_DIM), place).astype(jnp.bfloat16)
    k_rot = rotate(key.reshape(TOKENS, HEADS, HEAD_DIM), place).astype(jnp.bfloat16)
    v_b = value.astype(jnp.bfloat16).reshape(TOKENS, HEADS, HEAD_DIM)
    width = HEADS * HEAD_DIM
    cache_keys = jax.vmap(place_cache)(k_rot.reshape(GROUPS, GRP_TOK, width), cache_slot).reshape(TOKENS, width)
    cache_values = jax.vmap(place_cache)(v_b.reshape(GROUPS, GRP_TOK, width), cache_slot).reshape(TOKENS, width)
    shaped = (q_rot.reshape(GROUPS, GRP_TOK, HEADS, HEAD_DIM), k_rot.reshape(GROUPS, GRP_TOK, HEADS, HEAD_DIM), v_b.reshape(GROUPS, GRP_TOK, HEADS, HEAD_DIM), segment_ids)
    attended = lax.map(attend_group, shaped).reshape(TOKENS, width)
    attn_sum = block_sum(attended, w_out, N_HEAD)
    middle = (tokens.astype(jnp.float32) + attn_sum).astype(jnp.bfloat16)
    normed2 = norm_rows(middle, mlp_gain)
    gate = jnp.dot(normed2, w_gate, preferred_element_type=jnp.float32)
    up = jnp.dot(normed2, w_up, preferred_element_type=jnp.float32)
    hidden = (jax.nn.silu(gate) * up).astype(jnp.bfloat16)
    mlp_sum = block_sum(hidden, w_down, N_HEAD)
    layer_out = (middle.astype(jnp.float32) + mlp_sum).astype(jnp.bfloat16)
    return (layer_out, cache_keys, cache_values)
```

```python
import jax
import jax.numpy as jnp
import numpy as np
from jax import lax
from jax.experimental import pallas as pl
from jax.experimental.pallas import tpu as pltpu
from jax.sharding import PartitionSpec as P

MESH = pl.DeviceIdType.MESH
F32, BF16 = jnp.float32, jnp.bfloat16
NX, NZ, NY = 4, 8, 8
HEAD_DIM = 96
HALF = HEAD_DIM // 2
LANES = 128


def wrap(value, add, count):
    return lax.rem(value + (add + count), count)


def iota(shape, dim):
    return lax.broadcasted_iota(jnp.int32, shape, dim)


def nn(left, right):
    return jnp.dot(left, right, preferred_element_type=F32)


def nt(left, right):
    return lax.dot_general(left, right, (((1,), (1,)), ((), ())), preferred_element_type=F32)


def norm_rows(values, gain):
    scale = lax.rsqrt(jnp.mean(values * values, axis=-1, keepdims=True) + 1e-05)
    return (values * scale * gain).astype(BF16)


class Net:
    def __init__(self, send, recv):
        self.send, self.recv, self.copies = send, recv, []

    def put(self, src, dst, device):
        k = len(self.copies)
        copy = pltpu.make_async_remote_copy(
            src_ref=src,
            dst_ref=dst,
            send_sem=self.send.at[k],
            recv_sem=self.recv.at[k],
            device_id=device,
            device_id_type=MESH,
        )
        copy.start()
        self.copies.append(copy)
        return copy

    def drain(self):
        for copy in self.copies:
            copy.wait_send()


class Place:
    def __init__(self):
        group = lax.axis_index("group")
        self.y = lax.axis_index("head")
        self.core = lax.rem(group, 2)
        self.z = lax.rem(lax.div(group, 2), NZ)
        self.x = lax.div(group, 2 * NZ)

    def index(self, dx, dz, core):
        return (wrap(self.x, dx, NX) * NZ + wrap(self.z, dz, NZ)) * 2 + core

    def device(self, dx=0, dz=0, dy=0, sibling=False):
        core = 1 - self.core if sibling else self.core
        return (self.index(dx, dz, core), wrap(self.y, dy, NY))

    def neighbours(self):
        return (
            self.device(dx=1),
            self.device(dx=-1),
            self.device(dz=1),
            self.device(dz=-1),
            self.device(dy=1),
            self.device(dy=-1),
            self.device(sibling=True),
        )


def gather_weights(net, at, whole, rows):
    def block(dx, dz):
        start = pl.multiple_of(at.index(dx, dz, at.core) * rows, rows)
        return whole.at[pl.ds(start, rows), :]

    def push(ref, **where):
        return net.put(ref, ref, at.device(**where))

    siblings, across, second = [], {}, {}
    order = [0, -1, 1, -2, 2, -3, 3, -4]

    def arrived(dz):
        ref = block(0, dz)
        across[dz] = (push(ref, dx=1), push(ref, dx=-1))
        siblings.append(push(ref, sibling=True))

    def cross(dz):
        onward = order.index(dz) % 2
        for side in (0, 1):
            across[dz][side].wait_recv()
            ref = block(-1 if side == 0 else 1, dz)
            if side == onward:
                second[dz] = push(ref, dx=1 if side == 0 else -1)
            siblings.append(push(ref, sibling=True))

    def last(dz):
        second[dz].wait_recv()
        siblings.append(push(block(2, dz), sibling=True))

    own = block(0, 0)
    up, down = push(own, dz=1), push(own, dz=-1)
    arrived(0)
    yield
    todo_cross, todo_last = [0], []
    for step in range(1, 5):
        up.wait_recv()
        if step < 4:
            up = push(block(0, -step), dz=1)
        arrived(-step)
        fresh = [-step]
        if step < 4:
            down.wait_recv()
            if step < 3:
                down = push(block(0, step), dz=-1)
            arrived(step)
            fresh.append(step)
        yield
        for dz in todo_cross:
            cross(dz)
        for dz in todo_last:
            last(dz)
        todo_cross, todo_last = fresh, todo_cross
        yield
    for dz in todo_cross:
        cross(dz)
    yield
    for dz in todo_last + todo_cross:
        last(dz)
    yield
    for copy in siblings:
        copy.wait_recv()


def ways(chunk):
    return (4, 3) if chunk % 2 == 0 else (3, 4)


def gather_rows(net, at, whole, rows, chunks):
    width = whole.shape[1] // chunks

    def block(dy, chunk):
        start = pl.multiple_of(wrap(at.y, dy, NY) * rows, rows)
        return whole.at[pl.ds(start, rows), pl.ds(chunk * width, width)]

    flight = {}
    for step in range(1, 5):
        for chunk in range(chunks):
            for way in (0, 1):
                sign = 1 if way == 0 else -1
                if step > ways(chunk)[way]:
                    continue
                if step > 1:
                    flight[chunk, way].wait_recv()
                ref = block(-sign * (step - 1), chunk)
                flight[chunk, way] = net.put(ref, ref, at.device(dy=sign))
        yield
    for copy in flight.values():
        copy.wait_recv()


def sum_rows(net, at, terms, held, rows, chunks, finish):
    width = terms.shape[1] // chunks
    flight = {}

    def term(dy, columns):
        start = pl.multiple_of(wrap(at.y, dy, NY) * rows, rows)
        return terms.at[pl.ds(start, rows), columns]

    for step in range(1, 5):
        for chunk in range(chunks):
            columns = pl.ds(chunk * width, width)
            for way in (0, 1):
                sign, length = (1 if way == 0 else -1), ways(chunk)[way]
                if step > length:
                    continue
                mine = term(sign * (length - step + 1), columns)
                if step > 1:
                    flight[chunk, way].wait_recv()
                    slot = held.at[way, step - 2, :, columns]
                    slot[...] = (slot[...].astype(F32) + mine[...].astype(F32)).astype(BF16)
                    mine = slot
                flight[chunk, way] = net.put(mine, held.at[way, step - 1, :, columns], at.device(dy=sign))
        yield
    for chunk in range(chunks):
        columns = pl.ds(chunk * width, width)
        total = term(0, columns)[...].astype(F32)
        for way in (0, 1):
            flight[chunk, way].wait_recv()
            total = total + held[way, ways(chunk)[way] - 1, :, columns].astype(F32)
        finish(columns, total)


def key_columns():
    row, col = iota((2 * LANES, 2 * HEAD_DIM), 0), iota((2 * LANES, 2 * HEAD_DIM), 1)
    second = row >= LANES
    lane = jnp.where(second, row - LANES, row)
    target = lane + jnp.where(lane >= HALF, HALF, 0) + jnp.where(second, HALF, 0)
    return jnp.where((target == col) & (lane < HEAD_DIM), 1.0, 0.0).astype(BF16)


def value_columns():
    row, col = iota((2 * LANES, 2 * HEAD_DIM), 0), iota((2 * LANES, 2 * HEAD_DIM), 1)
    second = row >= LANES
    lane = jnp.where(second, row - LANES, row)
    target = lane + jnp.where(second, HEAD_DIM, 0)
    return jnp.where((target == col) & (lane < HEAD_DIM), 1.0, 0.0).astype(BF16)


def spare_columns():
    row, col = iota((2 * HEAD_DIM, 6 * LANES), 0), iota((2 * HEAD_DIM, 6 * LANES), 1)
    tile, lane = lax.shift_right_logical(col, 7), lax.bitwise_and(col, LANES - 1)
    return jnp.where((lane >= HEAD_DIM) & (row == tile * 32 + lane - HEAD_DIM), 1.0, 0.0).astype(BF16)


def eye(size):
    return jnp.where(iota((size, size), 0) == iota((size, size), 1), 1.0, 0.0).astype(BF16)


def pack_attention(wq, wk, wv, wo, dest):
    keys, values = key_columns(), value_columns()
    turned = nt(eye(wo.shape[1]), wo[...]).astype(BF16)
    spare = nn(turned, spare_columns())
    main = jnp.concatenate([nt(wq[...], keys), nt(wk[...], keys), nt(wv[...], values)], axis=1)
    dest[...] = (main + spare).astype(BF16)


def attention(qkv, seg, slot, freq, ck, cv):
    count = qkv.shape[0]
    row, col = iota((count, count), 0), iota((count, count), 1)
    seg_k = jnp.broadcast_to(seg[...], (count, count))
    seg_q = jnp.sum(jnp.where(row == col, seg_k, 0.0), axis=1, keepdims=True)
    first = jnp.sum(jnp.where(seg_k < seg_q, 1.0, 0.0), axis=1, keepdims=True)
    place = iota((count, 1), 0).astype(F32) - first
    angle = place * freq[...]
    cosine, sine = jnp.cos(angle), jnp.sin(angle)
    lane = iota((count, LANES), 1)
    live = lane < HEAD_DIM

    def tile(k):
        return qkv[:, k * LANES : (k + 1) * LANES]

    def rotated(u, w):
        turned = (u * cosine - w * sine, w * cosine + u * sine)
        return [jnp.where(live, part, 0.0).astype(BF16) for part in turned]

    queries = jnp.concatenate(rotated(tile(0), tile(1)), axis=1)
    key_parts = rotated(tile(2), tile(3))
    keys = jnp.concatenate(key_parts, axis=1)
    values = [jnp.where(live, tile(k), 0.0).astype(BF16) for k in (4, 5)]
    to_slot = jnp.where(row == jnp.broadcast_to(slot[...], (count, count)), 1.0, 0.0).astype(BF16)
    ck[...] = nn(nn(to_slot, keys).astype(BF16), key_columns()).astype(BF16)
    cv[...] = nn(nn(to_slot, jnp.concatenate(values, axis=1)).astype(BF16), value_columns()).astype(BF16)
    allowed = (seg_k == seg_q) & (col <= row)
    mixed = []
    for head in (0, 1):
        of_head = (lane >= head * HALF) & (lane < (head + 1) * HALF)
        key = jnp.concatenate([jnp.where(of_head, part, jnp.zeros_like(part)) for part in key_parts], axis=1)
        scores = nt(queries, key) * (1.0 / HEAD_DIM**0.5)
        scores = jnp.where(allowed, scores, -1e30)
        expo = jnp.exp(scores - jnp.max(scores, axis=1, keepdims=True))
        probs = (expo / jnp.sum(expo, axis=1, keepdims=True)).astype(BF16)
        mixed.append(nn(probs, values[head]).astype(BF16))
    return nn(jnp.concatenate(mixed, axis=1), value_columns()).astype(BF16)


def layer(
    tokens, gain, wq, wk, wv, wo, gain2, wg, wu, wd, seg, slot, freq,
    out, ck, cv,
    wa, wb, normed, normed2, qkv, spread, terms, terms2, hidden, held, held2, middle, send, recv,
):
    at = Place()
    net = Net(send, recv)
    rows, width = tokens.shape
    part, units = wq.shape[0], wg.shape[1]
    step = 256

    barrier = pltpu.get_barrier_semaphore()
    for device in at.neighbours():
        pl.semaphore_signal(barrier, inc=1, device_id=device, device_id_type=MESH)

    mine = pl.ds(pl.multiple_of(at.y * rows, rows), rows)
    shard = pl.ds(pl.multiple_of(at.index(0, 0, at.core) * part, part), part)
    normed[mine, :] = norm_rows(tokens[...].astype(F32), gain[...])
    pack_attention(wq, wk, wv, wo, wa.at[shard, :])
    pl.semaphore_wait(barrier, 7)

    weights = gather_weights(net, at, wa, part)
    for _ in gather_rows(net, at, normed, rows, 2):
        next(weights, None)
        next(weights, None)
    for _ in weights:
        pass

    wb[shard, pl.ds(0, units)] = wg[...]
    wb[shard, pl.ds(units, units)] = wu[...]
    wb[shard, pl.ds(2 * units, units)] = nt(eye(part), wd[...]).astype(BF16)
    weights = gather_weights(net, at, wb, part)
    next(weights)

    def project(k, carry):
        columns = pl.ds(pl.multiple_of(k * step, step), step)
        qkv[:, columns] = nn(normed[...], wa[:, columns])
        return carry

    lax.fori_loop(0, qkv.shape[1] // step, project, 0)
    next(weights)
    attended = attention(qkv, seg, slot, freq, ck, cv)
    spread[...] = nn(attended, spare_columns()).astype(BF16)

    def expand(k, carry):
        columns = pl.ds(pl.multiple_of(k * step, step), step)
        terms[:, columns] = nt(spread[...], wa[columns, :]).astype(BF16)
        return carry

    lax.fori_loop(0, width // step, expand, 0)
    next(weights)

    def add_attention(columns, total):
        middle[:, columns] = (tokens[:, columns].astype(F32) + total).astype(BF16)

    for _ in sum_rows(net, at, terms, held, rows, 2, add_attention):
        next(weights, None)
    normed2[mine, :] = norm_rows(middle[...].astype(F32), gain2[...])
    for _ in gather_rows(net, at, normed2, rows, 2):
        next(weights, None)
    for _ in weights:
        pass

    def gated(k, carry):
        first = pl.ds(pl.multiple_of(k * step, step), step)
        later = pl.ds(pl.multiple_of(k * step + units, step), step)
        gate = nn(normed2[...], wb[:, first])
        up = nn(normed2[...], wb[:, later])
        hidden[:, first] = (gate / (1.0 + jnp.exp(-gate)) * up).astype(BF16)
        return carry

    lax.fori_loop(0, units // step, gated, 0)

    def lower(k, carry):
        columns = pl.ds(pl.multiple_of(k * step, step), step)
        terms2[:, columns] = nt(hidden[...], wb[columns, pl.ds(2 * units, units)]).astype(BF16)
        return carry

    lax.fori_loop(0, width // step, lower, 0)

    def add_mlp(columns, total):
        out[:, columns] = (middle[:, columns].astype(F32) + total).astype(BF16)

    for _ in sum_rows(net, at, terms2, held2, rows, 2, add_mlp):
        pass
    net.drain()


def frequencies():
    lane = np.arange(LANES) % HALF
    return (10000.0 ** (-2.0 * lane / HEAD_DIM)).astype(np.float32)[None, :]


def per_device(
    tokens, attn_gain, w_query, w_key, w_value, w_out, mlp_gain, w_gate, w_up, w_down, segment_ids, cache_slot
):
    rows, width = tokens.shape
    heads = w_query.shape[1]
    units = w_gate.shape[1]
    count = rows * NY
    copies = 2 * 63 + 4 * 14
    vmem = pl.BlockSpec(memory_space=pltpu.VMEM)
    return pl.pallas_call(
        layer,
        name="layer",
        out_shape=(
            jax.ShapeDtypeStruct((rows, width), BF16),
            jax.ShapeDtypeStruct((count, heads), BF16),
            jax.ShapeDtypeStruct((count, heads), BF16),
        ),
        in_specs=[vmem] * 13,
        out_specs=(vmem,) * 3,
        scratch_shapes=[
            pltpu.VMEM((width, 6 * LANES), BF16),
            pltpu.VMEM((width, 3 * units), BF16),
            pltpu.VMEM((count, width), BF16),
            pltpu.VMEM((count, width), BF16),
            pltpu.VMEM((count, 6 * LANES), F32),
            pltpu.VMEM((count, 6 * LANES), BF16),
            pltpu.VMEM((count, width), BF16),
            pltpu.VMEM((count, width), BF16),
            pltpu.VMEM((count, units), BF16),
            pltpu.VMEM((2, 4, rows, width), BF16),
            pltpu.VMEM((2, 4, rows, width), BF16),
            pltpu.VMEM((rows, width), BF16),
            pltpu.SemaphoreType.DMA((copies,)),
            pltpu.SemaphoreType.DMA((copies,)),
        ],
        compiler_params=pltpu.CompilerParams(
            collective_id=0, has_side_effects=True, vmem_limit_bytes=56 * 2**20
        ),
    )(
        tokens,
        attn_gain[None, :],
        w_query,
        w_key,
        w_value,
        w_out,
        mlp_gain[None, :],
        w_gate,
        w_up,
        w_down,
        segment_ids.astype(F32),
        cache_slot,
        jnp.asarray(frequencies()),
    )


def solution(mesh):
    in_specs = (
        P(("group", "head"), None),
        P(),
        P("group", "head"),
        P("group", "head"),
        P("group", "head"),
        P("head", "group"),
        P(),
        P("group", "head"),
        P("group", "head"),
        P("head", "group"),
        P("group", None),
        P("group", None),
    )
    out_specs = (P(("group", "head"), None), P("group", "head"), P("group", "head"))
    return jax.shard_map(
        per_device, mesh=mesh, in_specs=in_specs, out_specs=out_specs, check_vma=False
    )
```

```python
import jax
import jax.numpy as jnp
import numpy as np
from jax import lax
from jax.experimental import pallas as pl
from jax.experimental.pallas import tpu as pltpu
from jax.sharding import PartitionSpec as P

MESH = pl.DeviceIdType.MESH
F32, BF16 = jnp.float32, jnp.bfloat16
NX, NZ, NY = 4, 8, 8
HEAD_DIM = 96
HALF = HEAD_DIM // 2
LANES = 128


def wrap(value, add, count):
    return lax.rem(value + (add + count), count)


def iota(shape, dim):
    return lax.broadcasted_iota(jnp.int32, shape, dim)


def nn(left, right):
    return jnp.dot(left, right, preferred_element_type=F32)


def nt(left, right):
    return lax.dot_general(left, right, (((1,), (1,)), ((), ())), preferred_element_type=F32)


def norm_rows(values, gain):
    scale = lax.rsqrt(jnp.mean(values * values, axis=-1, keepdims=True) + 1e-05)
    return (values * scale * gain).astype(BF16)


class Net:
    def __init__(self, send, recv):
        self.send, self.recv, self.count = send, recv, 0

    def put(self, src, dst, device, k=None):
        if k is None:
            k, self.count = self.count, self.count + 1
        copy = pltpu.make_async_remote_copy(
            src_ref=src,
            dst_ref=dst,
            send_sem=self.send,
            recv_sem=self.recv.at[k],
            device_id=device,
            device_id_type=MESH,
        )
        copy.start()
        return copy

    def landed(self, ref, k, device):
        pltpu.make_async_remote_copy(ref, ref, self.send, self.recv.at[k], device, MESH).wait_recv()

    def sent(self, ref, device):
        pltpu.make_async_remote_copy(ref, ref, self.send, self.recv.at[0], device, MESH).wait_send()


class Place:
    def __init__(self):
        group = lax.axis_index("group")
        self.y = lax.axis_index("head")
        self.core = lax.rem(group, 2)
        self.z = lax.rem(lax.div(group, 2), NZ)
        self.x = lax.div(group, 2 * NZ)

    def index(self, dx, dz, core):
        return (wrap(self.x, dx, NX) * NZ + wrap(self.z, dz, NZ)) * 2 + core

    def device(self, dx=0, dz=0, dy=0, sibling=False):
        core = 1 - self.core if sibling else self.core
        return (self.index(dx, dz, core), wrap(self.y, dy, NY))

    def neighbours(self):
        return (
            self.device(dx=1),
            self.device(dx=-1),
            self.device(dz=1),
            self.device(dz=-1),
            self.device(dy=1),
            self.device(dy=-1),
            self.device(sibling=True),
        )


def route(first):
    blocks = []
    for dx in (0, -1, 1, 2):
        up = 4 if first == "z" or dx in (0, 2) else 3
        for dz in range(-up, NZ - up):
            on = []
            if first == "x" or dx == 0:
                if dz <= 0 and -dz < up:
                    on.append((0, 1))
                if dz >= 0 and dz < NZ - 1 - up:
                    on.append((0, -1))
            if first == "z" or dz == 0:
                if dx == 0:
                    on += [(1, 0), (-1, 0)]
                elif dx == -1 and (first == "x" or dz % 2 == 0):
                    on.append((1, 0))
                elif dx == 1 and first == "z" and dz % 2 == 1:
                    on.append((-1, 0))
            later = abs(dx) if first == "z" else abs(dz)
            blocks.append(((abs(dx) + abs(dz), later), dx, dz, on))
    return [block[1:] for block in sorted(blocks, key=lambda block: block[0])]


def gather_weights(net, at, whole, rows):
    def block(dx, dz):
        start = pl.multiple_of(at.index(dx, dz, at.core) * rows, rows)
        return whole.at[pl.ds(start, rows), :]

    def name(dx, dz):
        return (dx % NX) * NZ + dz % NZ

    other = NX * NZ

    def handle(dx, dz, on):
        ref = block(dx, dz)
        if (dx, dz) != (0, 0):
            net.landed(ref, name(dx, dz), at.device(dx=1))
        for sx, sz in on:
            net.put(ref, ref, at.device(dx=sx, dz=sz), name(dx - sx, dz - sz))
        net.put(ref, ref, at.device(sibling=True), other)

    for pair in zip(route("z"), route("x")):
        for core in (0, 1):

            @pl.when(at.core == core)
            def _(todo=pair[core]):
                handle(*todo)

        yield
    count = whole.shape[0]
    net.landed(whole.at[pl.ds(0, count // 2), :], other, at.device(sibling=True))
    net.sent(whole.at[pl.ds(0, count - rows), :], at.device(sibling=True))


def ways(chunk):
    return (4, 3) if chunk % 2 == 0 else (3, 4)


def gather_rows(net, at, whole, rows, chunks):
    width = whole.shape[1] // chunks

    def block(dy, chunk):
        start = pl.multiple_of(wrap(at.y, dy, NY) * rows, rows)
        return whole.at[pl.ds(start, rows), pl.ds(chunk * width, width)]

    flight = {}
    for step in range(1, 5):
        for chunk in range(chunks):
            for way in (0, 1):
                sign = 1 if way == 0 else -1
                if step > ways(chunk)[way]:
                    continue
                if step > 1:
                    flight[chunk, way].wait_recv()
                ref = block(-sign * (step - 1), chunk)
                flight[chunk, way] = net.put(ref, ref, at.device(dy=sign))
            yield
    for copy in flight.values():
        copy.wait_recv()
    net.sent(whole.at[pl.ds(0, (NY - 1) * rows), :], at.device(dy=1))


def sum_rows(net, at, terms, held, rows, chunks, produce, consume):
    width = terms.shape[1] // chunks
    flight = {}

    def term(dy, columns):
        start = pl.multiple_of(wrap(at.y, dy, NY) * rows, rows)
        return terms.at[pl.ds(start, rows), columns]

    for step in range(1, 5):
        for chunk in range(chunks):
            columns = pl.ds(chunk * width, width)
            if step == 1:
                produce(chunk * width, width)
            for way in (0, 1):
                sign, length = (1 if way == 0 else -1), ways(chunk)[way]
                if step > length:
                    continue
                mine = term(sign * (length - step + 1), columns)
                if step > 1:
                    flight[chunk, way].wait_recv()
                    slot = held.at[way, step - 2, :, columns]
                    slot[...] = (slot[...].astype(F32) + mine[...].astype(F32)).astype(BF16)
                    mine = slot
                flight[chunk, way] = net.put(mine, held.at[way, step - 1, :, columns], at.device(dy=sign))
            yield
    for chunk in range(chunks):
        columns = pl.ds(chunk * width, width)
        total = term(0, columns)[...].astype(F32)
        for way in (0, 1):
            flight[chunk, way].wait_recv()
            total = total + held[way, ways(chunk)[way] - 1, :, columns].astype(F32)
        consume(columns, total)
        yield
    net.sent(terms.at[pl.ds(0, (NY - 1) * rows), :], at.device(dy=1))


def weave(main, side, each):
    for k, _ in enumerate(main):
        if k % each == each - 1:
            next(side, None)


def finish(steps):
    for _ in steps:
        pass


def key_columns():
    row, col = iota((2 * HEAD_DIM, 2 * LANES), 0), iota((2 * HEAD_DIM, 2 * LANES), 1)
    second = col >= LANES
    lane = jnp.where(second, col - LANES, col)
    source = lane + jnp.where(lane >= HALF, HALF, 0) + jnp.where(second, HALF, 0)
    return jnp.where((source == row) & (lane < HEAD_DIM), 1.0, 0.0).astype(BF16)


def value_columns():
    row, col = iota((2 * HEAD_DIM, 2 * LANES), 0), iota((2 * HEAD_DIM, 2 * LANES), 1)
    second = col >= LANES
    lane = jnp.where(second, col - LANES, col)
    source = lane + jnp.where(second, HEAD_DIM, 0)
    return jnp.where((source == row) & (lane < HEAD_DIM), 1.0, 0.0).astype(BF16)


def spare_columns():
    row, col = iota((2 * HEAD_DIM, 6 * LANES), 0), iota((2 * HEAD_DIM, 6 * LANES), 1)
    tile, lane = lax.shift_right_logical(col, 7), lax.bitwise_and(col, LANES - 1)
    return jnp.where((lane >= HEAD_DIM) & (row == tile * 32 + lane - HEAD_DIM), 1.0, 0.0).astype(BF16)


def pack_attention(wq, wk, wv, wo, dest):
    keys, values = key_columns(), value_columns()
    spare = nn(wo[...], spare_columns())
    main = jnp.concatenate([nn(wq[...], keys), nn(wk[...], keys), nn(wv[...], values)], axis=1)
    dest[...] = (main + spare).astype(BF16)


def attention(qkv, seg, slot, freq, ck, cv):
    count = qkv.shape[0]
    row, col = iota((count, count), 0), iota((count, count), 1)
    seg_k = jnp.broadcast_to(seg[...].astype(F32), (count, count))
    seg_q = jnp.sum(jnp.where(row == col, seg_k, 0.0), axis=1, keepdims=True)
    first = jnp.sum(jnp.where(seg_k < seg_q, 1.0, 0.0), axis=1, keepdims=True)
    place = iota((count, 1), 0).astype(F32) - first
    angle = place * freq[...]
    cosine, sine = jnp.cos(angle), jnp.sin(angle)
    lane = iota((count, LANES), 1)
    live = lane < HEAD_DIM

    def tile(k):
        return qkv[:, k * LANES : (k + 1) * LANES]

    def rotated(u, w):
        turned = (u * cosine - w * sine, w * cosine + u * sine)
        return [jnp.where(live, part, 0.0).astype(BF16) for part in turned]

    queries = jnp.concatenate(rotated(tile(0), tile(1)), axis=1)
    key_parts = rotated(tile(2), tile(3))
    keys = jnp.concatenate(key_parts, axis=1)
    values = [jnp.where(live, tile(k), 0.0).astype(BF16) for k in (4, 5)]
    to_slot = jnp.where(row == jnp.broadcast_to(slot[...], (count, count)), 1.0, 0.0).astype(BF16)
    ck[...] = nt(key_columns(), nn(to_slot, keys).astype(BF16)).astype(BF16)
    cv[...] = nt(value_columns(), nn(to_slot, jnp.concatenate(values, axis=1)).astype(BF16)).astype(BF16)
    allowed = (seg_k == seg_q) & (col <= row)
    mixed = []
    for head in (0, 1):
        of_head = (lane >= head * HALF) & (lane < (head + 1) * HALF)
        key = jnp.concatenate([jnp.where(of_head, part, jnp.zeros_like(part)) for part in key_parts], axis=1)
        scores = nt(queries, key) * (1.0 / HEAD_DIM**0.5)
        scores = jnp.where(allowed, scores, -1e30)
        expo = jnp.exp(scores - jnp.max(scores, axis=1, keepdims=True))
        probs = (expo / jnp.sum(expo, axis=1, keepdims=True)).astype(BF16)
        mixed.append(nn(probs, values[head]).astype(BF16))
    return nt(jnp.concatenate(mixed, axis=1), value_columns()).astype(BF16)


def layer(
    tokens, gain, wq, wk, wv, wo, gain2, wg, wu, wd, seg, slot, freq,
    out, ck, cv,
    wa, wb, normed, normed2, qkv, spread, terms, terms2, hidden, held, held2, middle, send, recv_w, recv_y,
):
    at = Place()
    rows, width = tokens.shape
    part, units = wq.shape[0], wg.shape[1]
    step, chunks = 256, 4
    nets = [Net(send.at[k], recv_w.at[k]) for k in range(2)] + [Net(send.at[2 + k], recv_y.at[k]) for k in range(4)]

    barrier = pltpu.get_barrier_semaphore()
    for device in at.neighbours():
        pl.semaphore_signal(barrier, inc=1, device_id=device, device_id_type=MESH)

    mine = pl.ds(pl.multiple_of(at.y * rows, rows), rows)
    shard = pl.ds(pl.multiple_of(at.index(0, 0, at.core) * part, part), part)
    normed[mine, :] = norm_rows(tokens[...].astype(F32), gain[...])
    pack_attention(wq, wk, wv, wo, wa.at[shard, :])
    wb[shard, pl.ds(0, units)] = wg[...]
    wb[shard, pl.ds(units, units)] = wu[...]
    wb[shard, pl.ds(2 * units, units)] = wd[...]
    pl.semaphore_wait(barrier, 7)

    weights = gather_weights(nets[0], at, wa, part)
    next(weights)
    weave(gather_rows(nets[2], at, normed, rows, chunks), weights, 1)
    finish(weights)

    weights = gather_weights(nets[1], at, wb, part)
    next(weights)

    def project(k, carry):
        columns = pl.ds(pl.multiple_of(k * step, step), step)
        qkv[:, columns] = nn(normed[...], wa[:, columns])
        return carry

    lax.fori_loop(0, qkv.shape[1] // step, project, 0)
    for _ in range(4):
        next(weights)
    attended = attention(qkv, seg, slot, freq, ck, cv)
    spread[...] = nn(attended, spare_columns()).astype(BF16)
    for _ in range(4):
        next(weights)

    def expand(start, size):
        def tile(k, carry):
            columns = pl.ds(pl.multiple_of(start + k * step, step), step)
            terms[:, columns] = nt(spread[...], wa[columns, :]).astype(BF16)
            return carry

        lax.fori_loop(0, size // step, tile, 0)

    def add_attention(columns, total):
        middle[:, columns] = (tokens[:, columns].astype(F32) + total).astype(BF16)

    weave(sum_rows(nets[3], at, terms, held, rows, chunks, expand, add_attention), weights, 2)
    normed2[mine, :] = norm_rows(middle[...].astype(F32), gain2[...])
    weave(gather_rows(nets[4], at, normed2, rows, chunks), weights, 1)
    finish(weights)

    def gated(k, carry):
        first = pl.ds(pl.multiple_of(k * step, step), step)
        later = pl.ds(pl.multiple_of(k * step + units, step), step)
        gate = nn(normed2[...], wb[:, first])
        up = nn(normed2[...], wb[:, later])
        hidden[:, first] = (gate / (1.0 + jnp.exp(-gate)) * up).astype(BF16)
        return carry

    lax.fori_loop(0, units // step, gated, 0)

    def lower(start, size):
        def tile(k, carry):
            columns = pl.ds(pl.multiple_of(start + k * step, step), step)
            terms2[:, columns] = nt(hidden[...], wb[columns, pl.ds(2 * units, units)]).astype(BF16)
            return carry

        lax.fori_loop(0, size // step, tile, 0)

    def add_mlp(columns, total):
        out[:, columns] = (middle[:, columns].astype(F32) + total).astype(BF16)

    finish(sum_rows(nets[5], at, terms2, held2, rows, chunks, lower, add_mlp))


def frequencies():
    lane = np.arange(LANES) % HALF
    return (10000.0 ** (-2.0 * lane / HEAD_DIM)).astype(np.float32)[None, :]


def per_device(
    tokens, attn_gain, w_query, w_key, w_value, w_out, mlp_gain, w_gate, w_up, w_down, segment_ids, cache_slot
):
    rows, width = tokens.shape
    heads = w_query.shape[1]
    units = w_gate.shape[1]
    count = rows * NY
    vmem = pl.BlockSpec(memory_space=pltpu.VMEM)
    layer_out, keys, values = pl.pallas_call(
        layer,
        name="layer",
        out_shape=(
            jax.ShapeDtypeStruct((rows, width), BF16),
            jax.ShapeDtypeStruct((heads, count), BF16),
            jax.ShapeDtypeStruct((heads, count), BF16),
        ),
        in_specs=[vmem] * 13,
        out_specs=(vmem,) * 3,
        scratch_shapes=[
            pltpu.VMEM((width, 6 * LANES), BF16),
            pltpu.VMEM((width, 3 * units), BF16),
            pltpu.VMEM((count, width), BF16),
            pltpu.VMEM((count, width), BF16),
            pltpu.VMEM((count, 6 * LANES), F32),
            pltpu.VMEM((count, 6 * LANES), BF16),
            pltpu.VMEM((count, width), BF16),
            pltpu.VMEM((count, width), BF16),
            pltpu.VMEM((count, units), BF16),
            pltpu.VMEM((2, 4, rows, width), BF16),
            pltpu.VMEM((2, 4, rows, width), BF16),
            pltpu.VMEM((rows, width), BF16),
            pltpu.SemaphoreType.DMA((6,)),
            pltpu.SemaphoreType.DMA((2, NX * NZ + 1)),
            pltpu.SemaphoreType.DMA((4, 28)),
        ],
        compiler_params=pltpu.CompilerParams(
            collective_id=0, has_side_effects=True, vmem_limit_bytes=56 * 2**20
        ),
    )(
        tokens,
        attn_gain[None, :],
        w_query,
        w_key,
        w_value,
        w_out.T,
        mlp_gain[None, :],
        w_gate,
        w_up,
        w_down.T,
        segment_ids,
        cache_slot,
        jnp.asarray(frequencies()),
    )
    return layer_out, keys.T, values.T


def solution(mesh):
    in_specs = (
        P(("group", "head"), None),
        P(),
        P("group", "head"),
        P("group", "head"),
        P("group", "head"),
        P("head", "group"),
        P(),
        P("group", "head"),
        P("group", "head"),
        P("head", "group"),
        P("group", None),
        P("group", None),
    )
    out_specs = (P(("group", "head"), None), P("group", "head"), P("group", "head"))
    return jax.shard_map(
        per_device, mesh=mesh, in_specs=in_specs, out_specs=out_specs, check_vma=False
    )
```

```python
import jax
import jax.numpy as jnp
import numpy as np
from jax import lax
from jax.experimental import pallas as pl
from jax.experimental.pallas import tpu as pltpu
from jax.sharding import PartitionSpec as P

MESH = pl.DeviceIdType.MESH
F32, BF16 = jnp.float32, jnp.bfloat16
NX, NZ, NY = 4, 8, 8
HEAD_DIM = 96
HALF = HEAD_DIM // 2
LANES = 128


def wrap(value, add, count):
    return lax.rem(value + (add + count), count)


def iota(shape, dim):
    return lax.broadcasted_iota(jnp.int32, shape, dim)


def nn(left, right):
    return jnp.dot(left, right, preferred_element_type=F32)


def nt(left, right):
    return lax.dot_general(left, right, (((1,), (1,)), ((), ())), preferred_element_type=F32)


def norm_rows(values, gain):
    scale = lax.rsqrt(jnp.mean(values * values, axis=-1, keepdims=True) + 1e-05)
    return (values * scale * gain).astype(BF16)


class Net:
    def __init__(self, send, recv):
        self.send, self.recv, self.count = send, recv, 0

    def put(self, src, dst, device, k=None):
        if k is None:
            k, self.count = self.count, self.count + 1
        copy = pltpu.make_async_remote_copy(
            src_ref=src,
            dst_ref=dst,
            send_sem=self.send,
            recv_sem=self.recv.at[k],
            device_id=device,
            device_id_type=MESH,
        )
        copy.start()
        return copy

    def landed(self, ref, k, device):
        pltpu.make_async_remote_copy(ref, ref, self.send, self.recv.at[k], device, MESH).wait_recv()

    def sent(self, ref, device):
        pltpu.make_async_remote_copy(ref, ref, self.send, self.recv.at[0], device, MESH).wait_send()


class Place:
    def __init__(self):
        group = lax.axis_index("group")
        self.y = lax.axis_index("head")
        self.core = lax.rem(group, 2)
        self.z = lax.rem(lax.div(group, 2), NZ)
        self.x = lax.div(group, 2 * NZ)

    def index(self, dx, dz, core):
        return (wrap(self.x, dx, NX) * NZ + wrap(self.z, dz, NZ)) * 2 + core

    def device(self, dx=0, dz=0, dy=0, sibling=False):
        core = 1 - self.core if sibling else self.core
        return (self.index(dx, dz, core), wrap(self.y, dy, NY))

    def neighbours(self):
        return (
            self.device(dx=1),
            self.device(dx=-1),
            self.device(dz=1),
            self.device(dz=-1),
            self.device(dx=2),
            self.device(dz=2),
            self.device(dz=-2),
            self.device(dy=1),
            self.device(dy=-1),
            self.device(sibling=True),
        )


def route(first, far):
    blocks = []
    for dx in (0, -1, 1, 2):
        up = 4 if first == "z" or dx in (0, 2) else 3
        for dz in range(-up, NZ - up):
            on = []
            if first == "z":
                if dx == 0:
                    if far:
                        on += {0: [(0, 1), (0, -1), (0, 2), (0, -2)], -2: [(0, 2), (0, 1)], 2: [(0, -1)]}.get(dz, [])
                    else:
                        on += [(0, 1)] * (-4 < dz <= 0) + [(0, -1)] * (0 <= dz < 3)
                    on += [(1, 0), (-1, 0)]
                elif dx == -1 and dz % 2 == 0:
                    on.append((1, 0))
                elif dx == 1 and dz % 2 == 1:
                    on.append((-1, 0))
                depth = ((abs(dz) + 1) // 2 if far else abs(dz)) + abs(dx)
            else:
                if (dx, dz) == (0, 0):
                    on += [(1, 0), (-1, 0), (2, 0)]
                if dz <= 0 and -dz < up:
                    on.append((0, 1))
                if dz >= 0 and dz < NZ - 1 - up:
                    on.append((0, -1))
                depth = (abs(dx) + 1) // 2 + abs(dz)
            later = abs(dx) if first == "z" else abs(dz)
            blocks.append(((depth, later), dx, dz, on))
    return [block[1:] for block in sorted(blocks, key=lambda block: block[0])]


def gather_weights(net, at, whole, rows, far):
    def block(dx, dz):
        start = pl.multiple_of(at.index(dx, dz, at.core) * rows, rows)
        return whole.at[pl.ds(start, rows), :]

    def name(dx, dz):
        return (dx % NX) * NZ + dz % NZ

    other = NX * NZ

    def handle(dx, dz, on):
        ref = block(dx, dz)
        if (dx, dz) != (0, 0):
            net.landed(ref, name(dx, dz), at.device(dx=1))
        for sx, sz in on:
            net.put(ref, ref, at.device(dx=sx, dz=sz), name(dx - sx, dz - sz))
        net.put(ref, ref, at.device(sibling=True), other)

    for pair in zip(route("z", far), route("x", far)):
        for core in (0, 1):

            @pl.when(at.core == core)
            def _(todo=pair[core]):
                handle(*todo)

        yield
    count = whole.shape[0]
    net.landed(whole.at[pl.ds(0, count // 2), :], other, at.device(sibling=True))
    net.sent(whole.at[pl.ds(0, count - rows), :], at.device(sibling=True))


def ways(chunk):
    return (4, 3) if chunk % 2 == 0 else (3, 4)


def gather_rows(net, at, whole, rows, chunks):
    width = whole.shape[1] // chunks

    def block(dy, chunk):
        start = pl.multiple_of(wrap(at.y, dy, NY) * rows, rows)
        return whole.at[pl.ds(start, rows), pl.ds(chunk * width, width)]

    flight = {}
    for step in range(1, 5):
        for chunk in range(chunks):
            for way in (0, 1):
                sign = 1 if way == 0 else -1
                if step > ways(chunk)[way]:
                    continue
                if step > 1:
                    flight[chunk, way].wait_recv()
                ref = block(-sign * (step - 1), chunk)
                flight[chunk, way] = net.put(ref, ref, at.device(dy=sign))
            yield
    for copy in flight.values():
        copy.wait_recv()
    net.sent(whole.at[pl.ds(0, (NY - 1) * rows), :], at.device(dy=1))


def sum_rows(net, at, terms, held, rows, chunks, produce, consume):
    width = terms.shape[1] // chunks
    flight = {}

    def term(dy, columns):
        start = pl.multiple_of(wrap(at.y, dy, NY) * rows, rows)
        return terms.at[pl.ds(start, rows), columns]

    for step in range(1, 5):
        for chunk in range(chunks):
            columns = pl.ds(chunk * width, width)
            if step == 1:
                produce(chunk * width, width)
            for way in (0, 1):
                sign, length = (1 if way == 0 else -1), ways(chunk)[way]
                if step > length:
                    continue
                mine = term(sign * (length - step + 1), columns)
                if step > 1:
                    flight[chunk, way].wait_recv()
                    slot = held.at[way, step - 2, :, columns]
                    slot[...] = (slot[...].astype(F32) + mine[...].astype(F32)).astype(BF16)
                    mine = slot
                flight[chunk, way] = net.put(mine, held.at[way, step - 1, :, columns], at.device(dy=sign))
            yield
    for chunk in range(chunks):
        columns = pl.ds(chunk * width, width)
        total = term(0, columns)[...].astype(F32)
        for way in (0, 1):
            flight[chunk, way].wait_recv()
            total = total + held[way, ways(chunk)[way] - 1, :, columns].astype(F32)
        consume(columns, total)
        yield
    net.sent(terms.at[pl.ds(0, (NY - 1) * rows), :], at.device(dy=1))


def weave(main, side, each):
    for _ in main:
        for _ in range(each):
            next(side, None)


def finish(steps):
    for _ in steps:
        pass


def key_columns():
    row, col = iota((2 * HEAD_DIM, 2 * LANES), 0), iota((2 * HEAD_DIM, 2 * LANES), 1)
    second = col >= LANES
    lane = jnp.where(second, col - LANES, col)
    source = lane + jnp.where(lane >= HALF, HALF, 0) + jnp.where(second, HALF, 0)
    return jnp.where((source == row) & (lane < HEAD_DIM), 1.0, 0.0).astype(BF16)


def value_columns():
    row, col = iota((2 * HEAD_DIM, 2 * LANES), 0), iota((2 * HEAD_DIM, 2 * LANES), 1)
    second = col >= LANES
    lane = jnp.where(second, col - LANES, col)
    source = lane + jnp.where(second, HEAD_DIM, 0)
    return jnp.where((source == row) & (lane < HEAD_DIM), 1.0, 0.0).astype(BF16)


def spare_columns():
    row, col = iota((2 * HEAD_DIM, 6 * LANES), 0), iota((2 * HEAD_DIM, 6 * LANES), 1)
    tile, lane = lax.shift_right_logical(col, 7), lax.bitwise_and(col, LANES - 1)
    return jnp.where((lane >= HEAD_DIM) & (row == tile * 32 + lane - HEAD_DIM), 1.0, 0.0).astype(BF16)


def pack_attention(wq, wk, wv, wo, dest):
    keys, values = key_columns(), value_columns()
    spare = nn(wo[...], spare_columns())
    main = jnp.concatenate([nn(wq[...], keys), nn(wk[...], keys), nn(wv[...], values)], axis=1)
    dest[...] = (main + spare).astype(BF16)


def attention(qkv, seg, slot, freq, ck, cv):
    count = qkv.shape[0]
    row, col = iota((count, count), 0), iota((count, count), 1)
    seg_k = jnp.broadcast_to(seg[...].astype(F32), (count, count))
    seg_q = jnp.sum(jnp.where(row == col, seg_k, 0.0), axis=1, keepdims=True)
    first = jnp.sum(jnp.where(seg_k < seg_q, 1.0, 0.0), axis=1, keepdims=True)
    place = iota((count, 1), 0).astype(F32) - first
    angle = place * freq[...]
    cosine, sine = jnp.cos(angle), jnp.sin(angle)
    lane = iota((count, LANES), 1)
    live = lane < HEAD_DIM

    def tile(k):
        return qkv[:, k * LANES : (k + 1) * LANES]

    def rotated(u, w):
        turned = (u * cosine - w * sine, w * cosine + u * sine)
        return [jnp.where(live, part, 0.0).astype(BF16) for part in turned]

    queries = jnp.concatenate(rotated(tile(0), tile(1)), axis=1)
    key_parts = rotated(tile(2), tile(3))
    keys = jnp.concatenate(key_parts, axis=1)
    values = [jnp.where(live, tile(k), 0.0).astype(BF16) for k in (4, 5)]
    to_slot = jnp.where(row == jnp.broadcast_to(slot[...], (count, count)), 1.0, 0.0).astype(BF16)
    ck[...] = nt(key_columns(), nn(to_slot, keys).astype(BF16)).astype(BF16)
    cv[...] = nt(value_columns(), nn(to_slot, jnp.concatenate(values, axis=1)).astype(BF16)).astype(BF16)
    allowed = (seg_k == seg_q) & (col <= row)
    mixed = []
    for head in (0, 1):
        of_head = (lane >= head * HALF) & (lane < (head + 1) * HALF)
        key = jnp.concatenate([jnp.where(of_head, part, jnp.zeros_like(part)) for part in key_parts], axis=1)
        scores = nt(queries, key) * (1.0 / HEAD_DIM**0.5)
        scores = jnp.where(allowed, scores, -1e30)
        expo = jnp.exp(scores - jnp.max(scores, axis=1, keepdims=True))
        probs = (expo / jnp.sum(expo, axis=1, keepdims=True)).astype(BF16)
        mixed.append(nn(probs, values[head]).astype(BF16))
    return nt(jnp.concatenate(mixed, axis=1), value_columns()).astype(BF16)


def layer(
    tokens, gain, wq, wk, wv, wo, gain2, wg, wu, wd, seg, slot, freq,
    out, ck, cv,
    wa, wb, normed, normed2, qkv, spread, terms, terms2, hidden, held, held2, middle, send, recv_w, recv_y,
):
    at = Place()
    rows, width = tokens.shape
    part, units = wq.shape[0], wg.shape[1]
    step, chunks = 256, 4
    nets = [Net(send.at[k], recv_w.at[k]) for k in range(2)] + [Net(send.at[2 + k], recv_y.at[k]) for k in range(4)]

    barrier = pltpu.get_barrier_semaphore()
    for device in at.neighbours():
        pl.semaphore_signal(barrier, inc=1, device_id=device, device_id_type=MESH)

    mine = pl.ds(pl.multiple_of(at.y * rows, rows), rows)
    shard = pl.ds(pl.multiple_of(at.index(0, 0, at.core) * part, part), part)
    normed[mine, :] = norm_rows(tokens[...].astype(F32), gain[...])
    pack_attention(wq, wk, wv, wo, wa.at[shard, :])
    wb[shard, pl.ds(0, units)] = wg[...]
    wb[shard, pl.ds(units, units)] = wu[...]
    wb[shard, pl.ds(2 * units, units)] = wd[...]
    pl.semaphore_wait(barrier, 10)

    weights = gather_weights(nets[0], at, wa, part, True)
    next(weights)
    weave(gather_rows(nets[2], at, normed, rows, chunks), weights, 2)
    finish(weights)
    weights = gather_weights(nets[1], at, wb, part, False)
    next(weights)


    def project(k, carry):
        columns = pl.ds(pl.multiple_of(k * step, step), step)
        qkv[:, columns] = nn(normed[...], wa[:, columns])
        return carry

    lax.fori_loop(0, qkv.shape[1] // step, project, 0)
    attended = attention(qkv, seg, slot, freq, ck, cv)
    spread[...] = nn(attended, spare_columns()).astype(BF16)

    def expand(start, size):
        def tile(k, carry):
            columns = pl.ds(pl.multiple_of(start + k * step, step), step)
            terms[:, columns] = nt(spread[...], wa[columns, :]).astype(BF16)
            return carry

        lax.fori_loop(0, size // step, tile, 0)

    def add_attention(columns, total):
        middle[:, columns] = (tokens[:, columns].astype(F32) + total).astype(BF16)

    weave(sum_rows(nets[3], at, terms, held, rows, chunks, expand, add_attention), weights, 1)
    normed2[mine, :] = norm_rows(middle[...].astype(F32), gain2[...])
    weave(gather_rows(nets[4], at, normed2, rows, chunks), weights, 1)
    finish(weights)

    def gated(k, carry):
        first = pl.ds(pl.multiple_of(k * step, step), step)
        later = pl.ds(pl.multiple_of(k * step + units, step), step)
        gate = nn(normed2[...], wb[:, first])
        up = nn(normed2[...], wb[:, later])
        hidden[:, first] = (gate / (1.0 + jnp.exp(-gate)) * up).astype(BF16)
        return carry

    lax.fori_loop(0, units // step, gated, 0)

    def lower(start, size):
        def tile(k, carry):
            columns = pl.ds(pl.multiple_of(start + k * step, step), step)
            terms2[:, columns] = nt(hidden[...], wb[columns, pl.ds(2 * units, units)]).astype(BF16)
            return carry

        lax.fori_loop(0, size // step, tile, 0)

    def add_mlp(columns, total):
        out[:, columns] = (middle[:, columns].astype(F32) + total).astype(BF16)

    finish(sum_rows(nets[5], at, terms2, held2, rows, chunks, lower, add_mlp))


def frequencies():
    lane = np.arange(LANES) % HALF
    return (10000.0 ** (-2.0 * lane / HEAD_DIM)).astype(np.float32)[None, :]


def per_device(
    tokens, attn_gain, w_query, w_key, w_value, w_out, mlp_gain, w_gate, w_up, w_down, segment_ids, cache_slot
):
    rows, width = tokens.shape
    heads = w_query.shape[1]
    units = w_gate.shape[1]
    count = rows * NY
    vmem = pl.BlockSpec(memory_space=pltpu.VMEM)
    layer_out, keys, values = pl.pallas_call(
        layer,
        name="layer",
        out_shape=(
            jax.ShapeDtypeStruct((rows, width), BF16),
            jax.ShapeDtypeStruct((heads, count), BF16),
            jax.ShapeDtypeStruct((heads, count), BF16),
        ),
        in_specs=[vmem] * 13,
        out_specs=(vmem,) * 3,
        scratch_shapes=[
            pltpu.VMEM((width, 6 * LANES), BF16),
            pltpu.VMEM((width, 3 * units), BF16),
            pltpu.VMEM((count, width), BF16),
            pltpu.VMEM((count, width), BF16),
            pltpu.VMEM((count, 6 * LANES), F32),
            pltpu.VMEM((count, 6 * LANES), BF16),
            pltpu.VMEM((count, width), BF16),
            pltpu.VMEM((count, width), BF16),
            pltpu.VMEM((count, units), BF16),
            pltpu.VMEM((2, 4, rows, width), BF16),
            pltpu.VMEM((2, 4, rows, width), BF16),
            pltpu.VMEM((rows, width), BF16),
            pltpu.SemaphoreType.DMA((6,)),
            pltpu.SemaphoreType.DMA((2, NX * NZ + 1)),
            pltpu.SemaphoreType.DMA((4, 28)),
        ],
        compiler_params=pltpu.CompilerParams(
            collective_id=0, has_side_effects=True, vmem_limit_bytes=56 * 2**20
        ),
    )(
        tokens,
        attn_gain[None, :],
        w_query,
        w_key,
        w_value,
        w_out.T,
        mlp_gain[None, :],
        w_gate,
        w_up,
        w_down.T,
        segment_ids,
        cache_slot,
        jnp.asarray(frequencies()),
    )
    return layer_out, keys.T, values.T


def solution(mesh):
    in_specs = (
        P(("group", "head"), None),
        P(),
        P("group", "head"),
        P("group", "head"),
        P("group", "head"),
        P("head", "group"),
        P(),
        P("group", "head"),
        P("group", "head"),
        P("head", "group"),
        P("group", None),
        P("group", None),
    )
    out_specs = (P(("group", "head"), None), P("group", "head"), P("group", "head"))
    return jax.shard_map(
        per_device, mesh=mesh, in_specs=in_specs, out_specs=out_specs, check_vma=False
    )
```

```python
import jax
import jax.numpy as jnp
import numpy as np
from jax import lax
from jax.experimental import pallas as pl
from jax.experimental.pallas import tpu as pltpu
from jax.sharding import PartitionSpec as P

MESH = pl.DeviceIdType.MESH
F32, BF16 = jnp.float32, jnp.bfloat16
NX, NZ, NY = 4, 8, 8
HEAD_DIM = 96
HALF = HEAD_DIM // 2
LANES = 128


def wrap(value, add, count):
    return lax.rem(value + (add + count), count)


def iota(shape, dim):
    return lax.broadcasted_iota(jnp.int32, shape, dim)


def nn(left, right):
    return jnp.dot(left, right, preferred_element_type=F32)


def nt(left, right):
    return lax.dot_general(left, right, (((1,), (1,)), ((), ())), preferred_element_type=F32)


def norm_rows(values, gain):
    scale = lax.rsqrt(jnp.mean(values * values, axis=-1, keepdims=True) + 1e-05)
    return (values * scale * gain).astype(BF16)


class Net:
    def __init__(self, send, recv):
        self.send, self.recv, self.count = send, recv, 0

    def put(self, src, dst, device, k=None):
        if k is None:
            k, self.count = self.count, self.count + 1
        copy = pltpu.make_async_remote_copy(
            src_ref=src,
            dst_ref=dst,
            send_sem=self.send,
            recv_sem=self.recv.at[k],
            device_id=device,
            device_id_type=MESH,
        )
        copy.start()
        return copy

    def landed(self, ref, k, device):
        pltpu.make_async_remote_copy(ref, ref, self.send, self.recv.at[k], device, MESH).wait_recv()

    def sent(self, ref, device):
        pltpu.make_async_remote_copy(ref, ref, self.send, self.recv.at[0], device, MESH).wait_send()


class Place:
    def __init__(self):
        group = lax.axis_index("group")
        self.y = lax.axis_index("head")
        self.core = lax.rem(group, 2)
        self.z = lax.rem(lax.div(group, 2), NZ)
        self.x = lax.div(group, 2 * NZ)

    def index(self, dx, dz, core):
        return (wrap(self.x, dx, NX) * NZ + wrap(self.z, dz, NZ)) * 2 + core

    def device(self, dx=0, dz=0, dy=0, sibling=False):
        core = 1 - self.core if sibling else self.core
        return (self.index(dx, dz, core), wrap(self.y, dy, NY))

    def neighbours(self):
        return (
            self.device(dx=1),
            self.device(dx=-1),
            self.device(dz=1),
            self.device(dz=-1),
            self.device(dx=2),
            self.device(dz=2),
            self.device(dz=-2),
            self.device(dy=1),
            self.device(dy=-1),
            self.device(sibling=True),
        )


def route(first, far):
    blocks = []
    for dx in (0, -1, 1, 2):
        up = 4 if first == "z" or dx in (0, 2) else 3
        for dz in range(-up, NZ - up):
            on = []
            if first == "z":
                if dx == 0:
                    if far:
                        on += {0: [(0, 1), (0, -1), (0, 2), (0, -2)], -2: [(0, 2), (0, 1)], 2: [(0, -1)]}.get(dz, [])
                    else:
                        on += [(0, 1)] * (-4 < dz <= 0) + [(0, -1)] * (0 <= dz < 3)
                    on += [(1, 0), (-1, 0)]
                elif dx == -1 and dz % 2 == 0:
                    on.append((1, 0))
                elif dx == 1 and dz % 2 == 1:
                    on.append((-1, 0))
                depth = ((abs(dz) + 1) // 2 if far else abs(dz)) + abs(dx)
            else:
                if (dx, dz) == (0, 0):
                    on += [(1, 0), (-1, 0), (2, 0)]
                if dz <= 0 and -dz < up:
                    on.append((0, 1))
                if dz >= 0 and dz < NZ - 1 - up:
                    on.append((0, -1))
                depth = (abs(dx) + 1) // 2 + abs(dz)
            later = abs(dx) if first == "z" else abs(dz)
            blocks.append(((depth, later), dx, dz, on))
    return [block[1:] for block in sorted(blocks, key=lambda block: block[0])]


def gather_weights(net, at, whole, rows, far):
    def block(dx, dz):
        start = pl.multiple_of(at.index(dx, dz, at.core) * rows, rows)
        return whole.at[pl.ds(start, rows), :]

    def name(dx, dz):
        return (dx % NX) * NZ + dz % NZ

    other = NX * NZ

    def handle(dx, dz, on):
        ref = block(dx, dz)
        if (dx, dz) != (0, 0):
            net.landed(ref, name(dx, dz), at.device(dx=1))
        for sx, sz in on:
            net.put(ref, ref, at.device(dx=sx, dz=sz), name(dx - sx, dz - sz))
        net.put(ref, ref, at.device(sibling=True), other)

    for pair in zip(route("z", far), route("x", far)):
        for core in (0, 1):

            @pl.when(at.core == core)
            def _(todo=pair[core]):
                handle(*todo)

        yield
    count = whole.shape[0]
    net.landed(whole.at[pl.ds(0, count // 2), :], other, at.device(sibling=True))
    net.sent(whole.at[pl.ds(0, count - rows), :], at.device(sibling=True))


def ways(chunk):
    return (4, 3) if chunk % 2 == 0 else (3, 4)


def gather_rows(net, at, whole, rows, chunks, prepare=None, arrived=None):
    width = whole.shape[1] // chunks

    def block(dy, chunk):
        start = pl.multiple_of(wrap(at.y, dy, NY) * rows, rows)
        return whole.at[pl.ds(start, rows), pl.ds(chunk * width, width)]

    flight, last = {}, []
    for step in range(1, 5):
        for chunk in range(chunks):
            if step == 1 and prepare is not None:
                prepare()
            for way in (0, 1):
                sign = 1 if way == 0 else -1
                if step > ways(chunk)[way]:
                    continue
                if step > 1:
                    flight.pop((chunk, way)).wait_recv()
                ref = block(-sign * (step - 1), chunk)
                flight[chunk, way] = net.put(ref, ref, at.device(dy=sign))
                if step == 4:
                    last.append(flight.pop((chunk, way)))
            yield
        if arrived is not None and step < 4:
            for dy in ((0,) if step == 1 else (step - 1, 1 - step)):
                arrived(dy)
    for copy in flight.values():
        copy.wait_recv()
    if arrived is not None:
        arrived(3)
        arrived(-3)
    for copy in last:
        copy.wait_recv()
    if arrived is not None:
        arrived(4)
    net.sent(whole.at[pl.ds(0, (NY - 1) * rows), :], at.device(dy=1))


def sum_rows(net, at, terms, held, rows, chunks, produce, consume):
    width = terms.shape[1] // chunks
    flight = {}

    def term(dy, columns):
        start = pl.multiple_of(wrap(at.y, dy, NY) * rows, rows)
        return terms.at[pl.ds(start, rows), columns]

    for step in range(1, 5):
        for chunk in range(chunks):
            columns = pl.ds(chunk * width, width)
            if step == 1:
                produce(chunk * width, width)
            for way in (0, 1):
                sign, length = (1 if way == 0 else -1), ways(chunk)[way]
                if step > length:
                    continue
                mine = term(sign * (length - step + 1), columns)
                if step > 1:
                    flight[chunk, way].wait_recv()
                    slot = held.at[way, step - 2, :, columns]
                    slot[...] = (slot[...].astype(F32) + mine[...].astype(F32)).astype(BF16)
                    mine = slot
                flight[chunk, way] = net.put(mine, held.at[way, step - 1, :, columns], at.device(dy=sign))
            yield
    for chunk in range(chunks):
        columns = pl.ds(chunk * width, width)
        total = term(0, columns)[...].astype(F32)
        for way in (0, 1):
            flight[chunk, way].wait_recv()
            total = total + held[way, ways(chunk)[way] - 1, :, columns].astype(F32)
        consume(columns, total)
        yield
    net.sent(terms.at[pl.ds(0, (NY - 1) * rows), :], at.device(dy=1))


def weave(main, side, each):
    for _ in main:
        for _ in range(each):
            next(side, None)


def finish(steps):
    for _ in steps:
        pass


def key_columns():
    row, col = iota((2 * HEAD_DIM, 2 * LANES), 0), iota((2 * HEAD_DIM, 2 * LANES), 1)
    second = col >= LANES
    lane = jnp.where(second, col - LANES, col)
    source = lane + jnp.where(lane >= HALF, HALF, 0) + jnp.where(second, HALF, 0)
    return jnp.where((source == row) & (lane < HEAD_DIM), 1.0, 0.0).astype(BF16)


def value_columns():
    row, col = iota((2 * HEAD_DIM, 2 * LANES), 0), iota((2 * HEAD_DIM, 2 * LANES), 1)
    second = col >= LANES
    lane = jnp.where(second, col - LANES, col)
    source = lane + jnp.where(second, HEAD_DIM, 0)
    return jnp.where((source == row) & (lane < HEAD_DIM), 1.0, 0.0).astype(BF16)


def spare_columns():
    row, col = iota((2 * HEAD_DIM, 6 * LANES), 0), iota((2 * HEAD_DIM, 6 * LANES), 1)
    tile, lane = lax.shift_right_logical(col, 7), lax.bitwise_and(col, LANES - 1)
    return jnp.where((lane >= HEAD_DIM) & (row == tile * 32 + lane - HEAD_DIM), 1.0, 0.0).astype(BF16)


def pack_attention(wq, wk, wv, wo, dest):
    keys, values = key_columns(), value_columns()
    spare = nn(wo[...], spare_columns())
    main = jnp.concatenate([nn(wq[...], keys), nn(wk[...], keys), nn(wv[...], values)], axis=1)
    dest[...] = (main + spare).astype(BF16)


def attention(qkv, seg, slot, freq, ck, cv):
    count = qkv.shape[0]
    row, col = iota((count, count), 0), iota((count, count), 1)
    seg_k = jnp.broadcast_to(seg[...].astype(F32), (count, count))
    seg_q = jnp.sum(jnp.where(row == col, seg_k, 0.0), axis=1, keepdims=True)
    first = jnp.sum(jnp.where(seg_k < seg_q, 1.0, 0.0), axis=1, keepdims=True)
    place = iota((count, 1), 0).astype(F32) - first
    angle = place * freq[...]
    cosine, sine = jnp.cos(angle), jnp.sin(angle)
    lane = iota((count, LANES), 1)
    live = lane < HEAD_DIM

    def tile(k):
        return qkv[:, k * LANES : (k + 1) * LANES]

    def rotated(u, w):
        turned = (u * cosine - w * sine, w * cosine + u * sine)
        return [jnp.where(live, part, 0.0).astype(BF16) for part in turned]

    queries = jnp.concatenate(rotated(tile(0), tile(1)), axis=1)
    key_parts = rotated(tile(2), tile(3))
    keys = jnp.concatenate(key_parts, axis=1)
    values = [jnp.where(live, tile(k), 0.0).astype(BF16) for k in (4, 5)]
    to_slot = jnp.where(row == jnp.broadcast_to(slot[...], (count, count)), 1.0, 0.0).astype(BF16)
    ck[...] = nt(key_columns(), nn(to_slot, keys).astype(BF16)).astype(BF16)
    cv[...] = nt(value_columns(), nn(to_slot, jnp.concatenate(values, axis=1)).astype(BF16)).astype(BF16)
    allowed = (seg_k == seg_q) & (col <= row)
    mixed = []
    for head in (0, 1):
        of_head = (lane >= head * HALF) & (lane < (head + 1) * HALF)
        key = jnp.concatenate([jnp.where(of_head, part, jnp.zeros_like(part)) for part in key_parts], axis=1)
        scores = nt(queries, key) * (1.0 / HEAD_DIM**0.5)
        scores = jnp.where(allowed, scores, -1e30)
        expo = jnp.exp(scores - jnp.max(scores, axis=1, keepdims=True))
        probs = (expo / jnp.sum(expo, axis=1, keepdims=True)).astype(BF16)
        mixed.append(nn(probs, values[head]).astype(BF16))
    return nt(jnp.concatenate(mixed, axis=1), value_columns()).astype(BF16)


def layer(
    tokens, gain, wq, wk, wv, wo, gain2, wg, wu, wd, seg, slot, freq,
    out, ck, cv,
    wa, wb, normed, normed2, qkv, spread, terms, terms2, hidden, held, held2, middles, done, keys, values, send, recv_w, recv_y, local,
):
    at = Place()
    rows, width = tokens.shape
    part, units = wq.shape[0], wg.shape[1]
    step, chunks = 256, 4
    nets = [Net(send.at[k], recv_w.at[k]) for k in range(2)] + [Net(send.at[2 + k], recv_y.at[k]) for k in range(4)]

    copies = []
    taken = iter(range(9))

    def keep(src, dst):
        copy = pltpu.make_async_copy(src, dst, local.at[next(taken)])
        copy.start()
        return copy

    barrier = pltpu.get_barrier_semaphore()
    for device in at.neighbours():
        pl.semaphore_signal(barrier, inc=1, device_id=device, device_id_type=MESH)

    mine = pl.ds(pl.multiple_of(at.y * rows, rows), rows)
    shard = pl.ds(pl.multiple_of(at.index(0, 0, at.core) * part, part), part)
    packed = [keep(ref, wb.at[shard, pl.ds(k * units, units)]) for k, ref in enumerate((wg, wu, wd))]
    normed[mine, :] = norm_rows(tokens[...].astype(F32), gain[...])
    pack_attention(wq, wk, wv, wo, wa.at[shard, :])
    pl.semaphore_wait(barrier, 10)

    weights = gather_weights(nets[0], at, wa, part, True)
    next(weights)
    weave(gather_rows(nets[2], at, normed, rows, chunks), weights, 2)
    finish(weights)
    for copy in packed:
        copy.wait()
    weights = gather_weights(nets[1], at, wb, part, False)
    next(weights)


    def project(k, carry):
        columns = pl.ds(pl.multiple_of(k * step, step), step)
        qkv[:, columns] = nn(normed[...], wa[:, columns])
        return carry

    lax.fori_loop(0, qkv.shape[1] // step, project, 0)
    attended = attention(qkv, seg, slot, freq, keys, values)
    copies += [keep(keys, ck), keep(values, cv)]
    spread[...] = nn(attended, spare_columns()).astype(BF16)

    def expand(start, size):
        def tile(k, carry):
            columns = pl.ds(pl.multiple_of(start + k * step, step), step)
            terms[:, columns] = nt(spread[...], wa[columns, :]).astype(BF16)
            return carry

        lax.fori_loop(0, size // step, tile, 0)

    def add_attention(columns, total):
        middles[mine, columns] = (tokens[:, columns].astype(F32) + total).astype(BF16)

    summed = sum_rows(nets[3], at, terms, held, rows, chunks, expand, add_attention)
    for _ in range(4 * chunks):
        next(summed)
        next(weights, None)

    def normalise(dy):
        block = pl.ds(pl.multiple_of(wrap(at.y, dy, NY) * rows, rows), rows)
        normed2[block, :] = norm_rows(middles[block, :].astype(F32), gain2[...])

    weave(gather_rows(nets[4], at, middles, rows, chunks, lambda: next(summed), normalise), weights, 1)
    finish(summed)
    finish(weights)

    def gated(k, carry):
        first = pl.ds(pl.multiple_of(k * step, step), step)
        later = pl.ds(pl.multiple_of(k * step + units, step), step)
        gate = nn(normed2[...], wb[:, first])
        up = nn(normed2[...], wb[:, later])
        hidden[:, first] = (gate / (1.0 + jnp.exp(-gate)) * up).astype(BF16)
        return carry

    lax.fori_loop(0, units // step, gated, 0)

    def lower(start, size):
        def tile(k, carry):
            columns = pl.ds(pl.multiple_of(start + k * step, step), step)
            terms2[:, columns] = nt(hidden[...], wb[columns, pl.ds(2 * units, units)]).astype(BF16)
            return carry

        lax.fori_loop(0, size // step, tile, 0)

    def add_mlp(columns, total):
        done[:, columns] = (middles[mine, columns].astype(F32) + total).astype(BF16)
        copies.append(keep(done.at[:, columns], out.at[:, columns]))

    finish(sum_rows(nets[5], at, terms2, held2, rows, chunks, lower, add_mlp))
    for copy in copies:
        copy.wait()


def frequencies():
    lane = np.arange(LANES) % HALF
    return (10000.0 ** (-2.0 * lane / HEAD_DIM)).astype(np.float32)[None, :]


def per_device(
    tokens, attn_gain, w_query, w_key, w_value, w_out, mlp_gain, w_gate, w_up, w_down, segment_ids, cache_slot
):
    rows, width = tokens.shape
    heads = w_query.shape[1]
    units = w_gate.shape[1]
    count = rows * NY
    vmem, hbm = pl.BlockSpec(memory_space=pltpu.VMEM), pl.BlockSpec(memory_space=pl.ANY)
    layer_out, keys, values = pl.pallas_call(
        layer,
        name="layer",
        out_shape=(
            jax.ShapeDtypeStruct((rows, width), BF16),
            jax.ShapeDtypeStruct((heads, count), BF16),
            jax.ShapeDtypeStruct((heads, count), BF16),
        ),
        in_specs=[vmem] * 7 + [hbm] * 3 + [vmem] * 3,
        out_specs=(hbm,) * 3,
        scratch_shapes=[
            pltpu.VMEM((width, 6 * LANES), BF16),
            pltpu.VMEM((width, 3 * units), BF16),
            pltpu.VMEM((count, width), BF16),
            pltpu.VMEM((count, width), BF16),
            pltpu.VMEM((count, 6 * LANES), F32),
            pltpu.VMEM((count, 6 * LANES), BF16),
            pltpu.VMEM((count, width), BF16),
            pltpu.VMEM((count, width), BF16),
            pltpu.VMEM((count, units), BF16),
            pltpu.VMEM((2, 4, rows, width), BF16),
            pltpu.VMEM((2, 4, rows, width), BF16),
            pltpu.VMEM((count, width), BF16),
            pltpu.VMEM((rows, width), BF16),
            pltpu.VMEM((heads, count), BF16),
            pltpu.VMEM((heads, count), BF16),
            pltpu.SemaphoreType.DMA((6,)),
            pltpu.SemaphoreType.DMA((2, NX * NZ + 1)),
            pltpu.SemaphoreType.DMA((4, 28)),
            pltpu.SemaphoreType.DMA((9,)),
        ],
        compiler_params=pltpu.CompilerParams(
            collective_id=0, has_side_effects=True, vmem_limit_bytes=56 * 2**20
        ),
    )(
        tokens,
        attn_gain[None, :],
        w_query,
        w_key,
        w_value,
        w_out.T,
        mlp_gain[None, :],
        w_gate,
        w_up,
        w_down.T,
        segment_ids,
        cache_slot,
        jnp.asarray(frequencies()),
    )
    return layer_out, keys.T, values.T


def solution(mesh):
    in_specs = (
        P(("group", "head"), None),
        P(),
        P("group", "head"),
        P("group", "head"),
        P("group", "head"),
        P("head", "group"),
        P(),
        P("group", "head"),
        P("group", "head"),
        P("head", "group"),
        P("group", None),
        P("group", None),
    )
    out_specs = (P(("group", "head"), None), P("group", "head"), P("group", "head"))
    return jax.shard_map(
        per_device, mesh=mesh, in_specs=in_specs, out_specs=out_specs, check_vma=False
    )
```
